32 devices in a mesh: member: 1, tile: 32 (over z, y, x, core).
Axes of the slice: x: 2, y: 2, z: 4, core: 2. Of those that a mesh axis runs over, the one named last changes fastest.
Arguments:
- forcing: bfloat16 [128, 8, 10, 128], P(('member', 'tile')), may hold values from -6 to 6
- ice_state: bfloat16 [1024, 128, 128], P(('member', 'tile')), may hold values from -6 to 6
- sensitivity: bfloat16 [1024, 128, 128], P(('member', 'tile')), may hold values from -6 to 6
- owner_device: int32 [1024, 4], P('tile'), may hold values from 0 to 31, all different within a row; in each aligned block of 32 rows (0 to 31, 32 to 63, ...) at most 8 rows name the same one
- panel_slot: int32 [1024, 4], P('tile'), may hold values from 0 to 3
- row_offset: int32 [1024, 4], P('tile'), may hold values from 0 to 7
- intersection_weight: float32 [1024, 4], P('tile'), may hold values from 0.2 to 1
- col_map: float32 [128, 128], replicated, may hold values from 0 to 1
- ocean_mask: int32 [1024, 128], P('tile'), may hold values 0 or 1
- lift_weight: bfloat16 [10, 128], replicated, may hold values from -1 to 1
- conv_weight: bfloat16 [3, 3, 3, 128, 128], replicated, may hold values from -0.1875 to 0.1875
- conv_bias: float32 [3, 128], replicated, may hold values from -3 to 3
Outputs:
- imitated: bfloat16 [1024, 128, 128], P(('member', 'tile'))
- state_grad: bfloat16 [1024, 128, 128], P(('member', 'tile'))
- forcing_grad: float32 [128, 8, 10, 128], P(('member', 'tile'))
The draws below stay inside these ranges and needn't reach their ends.
Inputs may be any that keep to these rules, and one draw needn't show every extreme that they name: `owner_device`: each ice row names 4 different owners; in the rows of one device no owner is named by more than 8 intersections, and that count is reached.
All inputs are finite; a program needn't handle non-finite values. No bound on the sum of `ocean_mask` on one device may be relied on, other than what follows from the above.
Results may differ from the reference program's by a relative error of at most 0.015.
Values may be sent and summed in bfloat16 or wider, within the bound.
A program may use at most 128 MiB of HBM per device.

```python
import math
import jax
import jax.numpy as jnp
import numpy as np
from jax import lax

C = 128
F = 10
L = 3
K = 4
PC = 128
COLS = 128
ROWS_DEV = 32
PR = 8
PAN_DEV = 4
ROWS = 1024
NPAN = 128
OWNERS = 32
CAP = 8


def draw_col_map(key, part):
    row_pos = jnp.arange(PC, dtype=jnp.int32)[:, None]
    col_pos = jnp.arange(COLS, dtype=jnp.int32)[None, :]
    centre = col_pos * PC // COLS
    inside = jnp.abs(row_pos - centre) <= 1
    values = jax.random.uniform(key, (PC, COLS), jnp.float32, 0.2, 1.0)
    return jnp.where(inside, values, jnp.float32(0.0)).astype(jnp.float32)


def place_ends(result, stream_key, smallest, high):
    shape = result.shape
    place = [jax.random.randint(jax.random.fold_in(stream_key, axis), (), 0, shape[axis]) for axis in range(len(shape))]
    result = result.at[tuple(place)].set(smallest)
    longest = shape.index(max(shape))
    place[longest] = (place[longest] + 1) % shape[longest]
    return result.at[tuple(place)].set(high)


def shard_levels(own_key, dims, pieces, low, top_value):
    level, own = 1.0, jax.random.fold_in(own_key, 6)
    for dim, shards_of in pieces:
        steps = jnp.exp(jax.random.uniform(jax.random.fold_in(own, dim), (shards_of,), jnp.float32, low / len(pieces), top_value / len(pieces)))
        level = level * jnp.repeat(steps, dims[dim] // shards_of).reshape([-1 if axis == dim else 1 for axis in range(len(dims))])
    return level


def assign_block(stream_key, own, number, rows, count, top, limit, slope):
    order = jax.random.permutation(stream_key, count)
    heavy_load, common = load_shares(count, rows * top, limit, slope, True), load_shares(count, rows * top, limit, slope, False)
    places = jnp.arange(count)

    def named(sizes, offset_by):
        used = int((sizes > 0).sum())
        fixed = max(1, used // 4)
        passed = fixed + (places - fixed + offset_by * (used - fixed)) % max(1, count - fixed)
        return jnp.zeros((count,), jnp.int32).at[order[jnp.where(places < fixed, places, passed)]].set(jnp.asarray(sizes, jnp.int32))

    sizes = jnp.where(number % 4 == 0, named(heavy_load, number // 4), named(common, number - number // 4 - 1))
    mixed = jax.random.permutation(jax.random.fold_in(own, 3), count)
    giver, taker = mixed[0:count // 2 * 2:2], mixed[1:count // 2 * 2:2]
    margin = jnp.minimum(sizes[giver] - 1, limit - sizes[taker]) // 2
    margin = jnp.where((giver == order[0]) | (taker == order[0]) | (sizes[taker] == 0), 0, jnp.maximum(margin, 0))
    passed = jax.random.randint(jax.random.fold_in(own, 4), (count // 2,), 0, 1 << 20) % (margin + 1)
    sizes = sizes.at[giver].add(-passed).at[taker].add(passed)
    items = jnp.searchsorted(jnp.cumsum(sizes), jnp.arange(rows * top), side="right").astype(jnp.int32)
    grid = items.reshape(top, rows).T
    grid = grid[jax.random.permutation(jax.random.fold_in(own, 1), rows)]
    offset_by = jax.random.randint(jax.random.fold_in(own, 2), (rows, 1), 0, top)
    return jnp.take_along_axis(grid, (jnp.arange(top)[None, :] + offset_by) % top, axis=1)


def load_shares(count, total, reach, lean, full):
    portions = [(1 << 20) // math.isqrt(rank ** lean) + 1 for rank in range(1, count + 1)]
    largest = reach if full else min(reach, max(-(-total // count), total * portions[0] // sum(portions)))
    least = 1 if total - largest >= count - 1 else 0
    given, surplus = [largest] + [least] * (count - 1), total - largest - least * (count - 1)
    while surplus > 0:
        free = [i for i in range(1, count) if given[i] < largest] or [i for i in range(1, count) if given[i] < reach]
        mass, left = sum([portions[i] for i in free]), surplus
        for i in free:
            addition = min(reach - given[i], max(1, left * portions[i] // mass), surplus)
            given[i] = given[i] + addition
            surplus = surplus - addition
    return np.array(given)


def scatter_about(own_key, shape, deviation, limit, cuts=(), kind=jnp.bfloat16):
    array = jax.random.normal(own_key, shape, jnp.float32) * deviation
    if len(cuts) > 0:
        array = shard_levels(own_key, shape, cuts, -0.22, 0.18) * array
    return jnp.clip(array, min=-limit, max=limit).astype(kind)


def setup_inputs(seed: int = 0, part: int = 0) -> dict:
    key_of = jax.random.split(jax.random.key(seed), 13)
    own_keys = jax.random.split(jax.random.fold_in(key_of[12], part), 13)
    forcing = scatter_about(own_keys[0], (NPAN, PR, F, PC), 1.0, 6.0, ((0, 32),))
    ice_state = scatter_about(own_keys[1], (ROWS, COLS, C), 1.0, 6.0, ((0, 32),))
    sensitivity = scatter_about(own_keys[2], (ROWS, COLS, C), 1.0, 6.0, ((0, 32),))
    owner_device_keys = jax.random.split(jax.random.fold_in(key_of[3], 1), ROWS // ROWS_DEV)
    owner_device_turns = jax.random.permutation(jax.random.fold_in(key_of[3], 3), ROWS // ROWS_DEV)
    owner_device = jax.vmap(lambda own, number: assign_block(jax.random.fold_in(key_of[3], 2), own, number, ROWS_DEV, OWNERS, K, CAP, 2))(owner_device_keys, owner_device_turns).reshape((ROWS, K))
    panel_slot = place_ends(jax.random.randint(key_of[4], (ROWS, K), 0, PAN_DEV), jax.random.fold_in(key_of[4], 1), 0, PAN_DEV - 1).astype(jnp.int32)
    row_offset = place_ends(jax.random.randint(key_of[5], (ROWS, K), 0, PR), jax.random.fold_in(key_of[5], 1), 0, PR - 1).astype(jnp.int32)
    intersection_weight = jnp.clip(jnp.exp(math.log(1.0) - 1.609438 * jax.random.uniform(key_of[6], (ROWS, K), jnp.float32) ** shard_levels(key_of[6], (ROWS, K), ((0, 32),), -0.2, 0.2)), 0.2, 1.0)
    col_map = draw_col_map(jax.random.fold_in(key_of[12], 71), part)
    ocean_mask = place_ends((jax.random.randint(key_of[8], (ROWS, COLS), 0, 4) < 3).astype(jnp.int32), jax.random.fold_in(key_of[8], 1), 0, 1)
    lift_weight = scatter_about(key_of[9], (F, C), (4 * F) ** -0.5, 1.0)
    conv_weight = scatter_about(key_of[10], (L, 3, 3, C, C), (9 * C) ** -0.5, 0.1875)
    conv_bias = scatter_about(key_of[11], (L, C), 0.5, 3.0, (), jnp.float32)
    return {"forcing": forcing, "ice_state": ice_state, "sensitivity": sensitivity, "owner_device": owner_device, "panel_slot": panel_slot, "row_offset": row_offset, "intersection_weight": intersection_weight, "col_map": col_map, "ocean_mask": ocean_mask, "lift_weight": lift_weight, "conv_weight": conv_weight, "conv_bias": conv_bias}


def convolve(field, kernel):
    return lax.conv_general_dilated(field[None].astype(jnp.float32), kernel.astype(jnp.float32), (1, 1), ((1, 1), (1, 1)), dimension_numbers=("NHWC", "HWIO", "NHWC"), precision=lax.Precision.HIGHEST)[0]


def reference(forcing, ice_state, sensitivity, owner_device, panel_slot, row_offset, intersection_weight, col_map, ocean_mask, lift_weight, conv_weight, conv_bias):
    highest = lax.Precision.HIGHEST
    flat_panels = forcing.reshape(NPAN * PR, F, PC)
    global_row = ((owner_device * PAN_DEV + panel_slot) * PR + row_offset).astype(jnp.int32)
    picked = flat_panels[global_row].astype(jnp.float32)
    mapped = jnp.einsum("rkfp,pc->rkfc", picked, col_map, precision=highest)
    ice_forcing = jnp.sum(intersection_weight[:, :, None, None] * mapped, axis=1).astype(jnp.bfloat16)
    lifted = jnp.einsum("rfc,fh->rch", ice_forcing.astype(jnp.float32), lift_weight.astype(jnp.float32), precision=highest)
    ocean_cells = ocean_mask.astype(jnp.float32)[:, :, None]
    hidden = ice_state
    tangents = []
    for layer_index in range(L):
        if layer_index == 1:
            hidden = (hidden.astype(jnp.float32) + lifted).astype(jnp.bfloat16)
        tangent = jnp.tanh(convolve(hidden, conv_weight[layer_index]) + conv_bias[layer_index])
        tangents.append(tangent)
        hidden = (hidden.astype(jnp.float32) + ocean_cells * tangent).astype(jnp.bfloat16)
    imitated = hidden
    adjoint = sensitivity.astype(jnp.float32)
    force_grad = jnp.zeros((ROWS, F, COLS), jnp.float32)
    for layer_index in reversed(range(L)):
        tangent = tangents[layer_index]
        delta_act = (adjoint * ocean_cells * (1.0 - tangent * tangent)).astype(jnp.bfloat16)
        flipped = jnp.flip(conv_weight[layer_index], (0, 1)).transpose(0, 1, 3, 2)
        adjoint = adjoint + convolve(delta_act, flipped)
        if layer_index == 1:
            force_grad = jnp.einsum("rch,fh->rfc", adjoint, lift_weight.astype(jnp.float32), precision=highest)
    projected = jnp.einsum("rfc,pc->rfp", force_grad, col_map, precision=highest)
    row_terms = intersection_weight[:, :, None, None] * projected[:, None]
    forcing_grad = jnp.zeros((NPAN * PR, F, PC), jnp.float32).at[global_row.reshape(-1)].add(row_terms.reshape(ROWS * K, F, PC))
    return imitated, adjoint.astype(jnp.bfloat16), forcing_grad.reshape(NPAN, PR, F, PC)
```

```python
import functools

import jax
import jax.numpy as jnp
from jax import lax
from jax.experimental import pallas as pl
from jax.experimental.pallas import tpu as pltpu
from jax.sharding import PartitionSpec as P

F = 10
K = 4
ROWS_DEV = 32
FP = 16
HALF = 640
BLK = 16
E = 48
f32, bf16 = jnp.float32, jnp.bfloat16


def dot(a, b, ca=1, cb=0):
    return lax.dot_general(a, b, (((ca,), (cb,)), ((), ())), preferred_element_type=f32)


def iota(shape, dim):
    return lax.broadcasted_iota(jnp.int32, shape, dim)


def remote(src, dst, send, recv, target):
    return pltpu.make_async_remote_copy(
        src_ref=src, dst_ref=dst, send_sem=send, recv_sem=recv,
        device_id={"tile": target}, device_id_type=pl.DeviceIdType.MESH,
    )


def enter(n, me):
    barrier = pltpu.get_barrier_semaphore()

    def greet(step, carry):
        pl.semaphore_signal(
            barrier, inc=1, device_id={"tile": lax.rem(me + step, n)},
            device_id_type=pl.DeviceIdType.MESH,
        )
        return carry

    lax.fori_loop(1, n, greet, 0)
    pl.semaphore_wait(barrier, n - 1)


def block(ref, p):
    return ref.at[pl.ds(pl.multiple_of(p * BLK, BLK), BLK)]


def exchange(n, me, src, dst, send, recv, start, wait):
    def begin(step, carry):
        to = lax.rem(me + step, n)
        remote(block(src, to), block(dst, me), send.at[step], recv.at[step], to).start()
        return carry

    def finish(step, carry):
        to = lax.rem(me + step, n)
        source = lax.rem(me + n - step, n)
        remote(block(src, to), block(dst, source), send.at[step], recv.at[step], to).wait()
        return carry

    if start:
        lax.fori_loop(1, n, begin, 0)
        mine = pl.ds(pl.multiple_of(me * BLK, BLK), BLK)
        dst[mine, :] = src[mine, :]
    if wait:
        lax.fori_loop(1, n, finish, 0)


def gather_kernel(
    n, ice, sens, ocean, own_c, own_r, loc_c, w_c, forc,
    pre_out, oh_out, w2_out, iceh, sensh, och,
    oh_send, oh_recv, f_send, f_recv, pre, prex,
    s1, r1, s2, r2, s3, r3,
):
    me = lax.axis_index("tile")
    right, left = lax.rem(me + 1, n), lax.rem(me + n - 1, n)
    nb = n * BLK
    nk = ROWS_DEV * K
    enter(n, me)
    own = own_c[...]
    same = own == own_r[...]
    earlier = iota((nk, nk), 1) < iota((nk, nk), 0)
    rank = jnp.sum(jnp.where(same & earlier, 1.0, 0.0), axis=1, keepdims=True).astype(jnp.int32)
    col = own * BLK + rank
    lane = iota((nk, nb), 1)
    pa = jnp.where(col == lane, 1.0, 0.0)
    pb = jnp.where(col + 8 == lane, 1.0, 0.0)
    low = iota((nk, 128), 1)
    la = jnp.where(loc_c[...] == low, 1.0, 0.0)
    lb = jnp.where(loc_c[...] + ROWS_DEV == low, 1.0, 0.0)
    oh = dot(pa.astype(bf16), la.astype(bf16), 0, 0) + dot(pb.astype(bf16), lb.astype(bf16), 0, 0)
    oh_send[...] = oh.astype(bf16)
    exchange(n, me, oh_send, oh_recv, s1, r1, True, False)
    halos = []
    for i, (src, dst, rows) in enumerate(((ice, iceh, 6), (sens, sensh, 3), (ocean, och, 8))):
        halos.append(remote(src.at[pl.ds(ROWS_DEV - rows, rows)], dst.at[0], s3.at[2 * i], r3.at[2 * i], right))
        halos.append(remote(src.at[pl.ds(0, rows)], dst.at[1], s3.at[2 * i + 1], r3.at[2 * i + 1], left))
    w = w_c[...]
    rows = iota((ROWS_DEV, nk), 0)
    cols = iota((ROWS_DEV, nk), 1)
    pick = jnp.where((cols >= rows * K) & (cols < rows * K + K), 1.0, 0.0).astype(bf16)
    wa = dot(pick, (pa * w).astype(bf16))
    wb = dot(pick, (pb * w).astype(bf16))
    w2 = jnp.concatenate([wa, wb], axis=0).astype(bf16)
    w2_out[...] = w2
    exchange(n, me, oh_send, oh_recv, s1, r1, False, True)
    got = oh_recv[...]
    oh_out[...] = got
    f_send[...] = dot(got[:, : 2 * ROWS_DEV], forc[...]).astype(bf16)
    exchange(n, me, f_send, f_recv, s2, r2, True, False)
    for copy in halos:
        copy.start()
    exchange(n, me, f_send, f_recv, s2, r2, False, True)
    pre[...] = dot(w2, f_recv[...]).astype(bf16)
    edges = []
    for half in range(2):
        at = half * 64
        low_rows = pre.at[pl.ds(half * ROWS_DEV, 16)]
        high_rows = pre.at[pl.ds(half * ROWS_DEV + 16, 16)]
        edges.append(remote(high_rows, prex.at[pl.ds(at, 16)], s3.at[6 + 2 * half], r3.at[6 + 2 * half], right))
        edges.append(remote(low_rows, prex.at[pl.ds(at + 48, 16)], s3.at[7 + 2 * half], r3.at[7 + 2 * half], left))
        prex[pl.ds(at + 16, ROWS_DEV), :] = pre[pl.ds(half * ROWS_DEV, ROWS_DEV), :]
    for copy in edges:
        copy.start()
    for copy in halos:
        copy.wait()
    for copy in edges:
        copy.wait()
    pre_out[...] = prex[...]


def layers_kernel(
    n, ice, sens, ocean, iceh, sensh, och, pre, col_map, lift, cw, cb, w2,
    img, sg, terms,
    xa, xb, s0, s1, s2, mask, g, h3, wf, wb, oc, icr, fg, pr2,
):
    me = lax.axis_index("tile")
    keep_low = jnp.where(me == 0, 0.0, 1.0)
    keep_high = jnp.where(me == n - 1, 0.0, 1.0)
    rows = iota((128, 128), 0)
    diag = jnp.where(rows == iota((128, 128), 1), 1.0, 0.0)
    ones = jnp.ones((128, 128), bf16)
    not_first = rows > 0
    not_last = rows < 127

    def put(dst, pair, half, v):
        at = half * 384
        dst[pair, :, at : at + 128] = jnp.where(not_first, pltpu.roll(v, 1, 0), 0.0).astype(bf16)
        dst[pair, :, at + 128 : at + 256] = v.astype(bf16)
        dst[pair, :, at + 256 : at + 384] = jnp.where(not_last, pltpu.roll(v, 127, 0), 0.0).astype(bf16)

    oc[0:8, :] = och[0].astype(f32) * keep_low
    oc[8:40, :] = ocean[...].astype(f32)
    oc[40:48, :] = och[1].astype(f32) * keep_high

    def spread(e, carry):
        mask[e] = dot((diag * oc[pl.ds(e, 1), :]).astype(bf16), ones)
        return carry

    lax.fori_loop(2, 46, spread, 0)

    for i in range(6):
        put(xa, (2 + i) // 2, i % 2, iceh[0, i].astype(f32) * keep_low)
        put(xa, (40 + i) // 2, i % 2, iceh[1, i].astype(f32) * keep_high)

    def fill(q, carry):
        put(xa, q + 4, 0, ice[2 * q].astype(f32))
        put(xa, q + 4, 1, ice[2 * q + 1].astype(f32))
        return carry

    lax.fori_loop(0, ROWS_DEV // 2, fill, 0)
    zero = jnp.zeros((128, 384), bf16)
    xb[1, :, 0:384] = zero
    xb[22, :, 384:768] = zero
    for i in range(3):
        g[5 + i] = sensh[0, i].astype(f32)
        g[40 + i] = sensh[1, i].astype(f32)
    g[43] = jnp.zeros((128, 128), f32)
    g[44] = jnp.zeros((128, 128), f32)

    def fill_g(r, carry):
        g[r + 8] = sens[r].astype(f32)
        return carry

    lax.fori_loop(0, ROWS_DEV, fill_g, 0)

    icr[...] = jnp.zeros_like(icr)
    cm = col_map[...].astype(bf16)
    ext = iota((64, 128), 0)
    low_edge = jnp.where(ext < 16, keep_low, 1.0)
    edge = low_edge * jnp.where(ext >= 48, keep_high, 1.0)
    for half in range(2):
        for i in range(5):
            x = pre[half * 64 : half * 64 + 64, i * 128 : i * 128 + 128]
            icr[:, half * 5 + i, :] = dot(x, cm) * edge
    lift16 = lift[...]

    for j in range(4):
        for s in range(2):
            if not 0 <= j - s <= 2:
                wf[j * 384 : j * 384 + 384, s * 128 : s * 128 + 128] = jnp.zeros((384, 128), bf16)
                wb[s * 128 : s * 128 + 128, j * 384 : j * 384 + 384] = jnp.zeros((128, 384), bf16)

    def set_forward(layer):
        for j in range(4):
            for s in range(2):
                if 0 <= j - s <= 2:
                    for b in range(3):
                        at = j * 384 + b * 128
                        wf[at : at + 128, s * 128 : s * 128 + 128] = cw[layer * 9 + (j - s) * 3 + b]

    def set_backward(layer):
        for j in range(4):
            for s in range(2):
                if 0 <= j - s <= 2:
                    for b in range(3):
                        at = j * 384 + b * 128
                        wb[s * 128 : s * 128 + 128, at : at + 128] = cw[layer * 9 + (2 - j + s) * 3 + 2 - b]

    def run(x, q_first, pairs, count, forward, finish):
        def chunk(c, carry):
            q0 = q_first + c * pairs
            left = x[pl.ds(q0, pairs)].reshape(pairs * 128, 768)
            right = x[pl.ds(q0 + 1, pairs)].reshape(pairs * 128, 768)
            if forward:
                acc = dot(left, wf[0:768, :]) + dot(right, wf[768:1536, :])
            else:
                acc = dot(left, wb[:, 0:768], 1, 1) + dot(right, wb[:, 768:1536], 1, 1)
            for i in range(pairs):
                for s in range(2):
                    part = acc[i * 128 : i * 128 + 128, s * 128 : s * 128 + 128]
                    finish(2 * (q0 + i) + 1 + s, q0 + i + s, 1 - s, part)
            return carry

        lax.fori_loop(0, count, chunk, 0)

    def middle(x, pair, half):
        return x[pair, :, half * 384 + 128 : half * 384 + 256].astype(f32)

    def forward_step(layer, x, keep):
        bias = cb[layer : layer + 1, :]

        def step(e, pair, half, acc):
            t = jnp.tanh(acc + bias)
            m = mask[e]
            keep[e] = m * (1.0 - t * t)
            return (middle(x, pair, half) + m * t).astype(bf16)

        return step

    step0, step1, step2 = forward_step(0, xa, s0), forward_step(1, xb, s1), forward_step(2, xa, s2)

    def finish0(e, pair, half, acc):
        h = step0(e, pair, half, acc).astype(f32)
        lifted = dot(icr[e + 8].astype(bf16), lift16, 0, 0)
        put(xb, pair, half, h + lifted)

    def finish1(e, pair, half, acc):
        put(xa, pair, half, step1(e, pair, half, acc).astype(f32))

    def finish2(e, pair, half, acc):
        h3[e] = step2(e, pair, half, acc)
        put(xb, pair, half, g[e] * s2[e])

    def back2(e, pair, half, acc):
        total = g[e] + acc
        g[e] = total
        put(xa, pair, half, total * s1[e])

    def back1(e, pair, half, acc):
        total = g[e] + acc
        g[e] = total
        put(xb, pair, half, total * s0[e])

    def back0(e, pair, half, acc):
        g[e] = g[e] + acc

    set_forward(0)
    run(xa, 1, 7, 3, True, finish0)
    set_forward(1)
    run(xb, 1, 7, 3, True, finish1)
    set_forward(2)
    run(xa, 2, 5, 4, True, finish2)
    img[...] = h3[8:40]
    set_backward(2)
    run(xb, 2, 5, 4, False, back2)
    set_backward(1)
    run(xa, 3, 6, 3, False, back1)

    def project(r, carry):
        fg[r] = dot(lift16, g[r + 8].astype(bf16), 1, 1)
        return carry

    lax.fori_loop(0, ROWS_DEV, project, 0)
    fg[...] = dot(fg[...].reshape(ROWS_DEV * FP, 128).astype(bf16), cm, 1, 1).reshape(ROWS_DEV, FP, 128)
    for half in range(2):
        for i in range(5):
            pr2[half * 32 : half * 32 + 32, i * 128 : i * 128 + 128] = fg[:, half * 5 + i, :].astype(bf16)
    terms[...] = dot(w2[...], pr2[...], 0, 0).astype(bf16)

    set_backward(0)
    run(xb, 3, 6, 3, False, back0)
    sg[...] = g[8:40].astype(bf16)


def return_kernel(n, terms, oh, out, recv, ss, rs):
    me = lax.axis_index("tile")
    enter(n, me)
    exchange(n, me, terms, recv, ss, rs, True, True)
    out[...] = dot(oh[:, : 2 * ROWS_DEV], recv[...], 0, 0)


def call(kernel, outs, scratch, ins, collective=None):
    params = dict(vmem_limit_bytes=50 * 1024 * 1024)
    if collective is not None:
        params.update(collective_id=collective, has_side_effects=True)
    vmem = pl.BlockSpec(memory_space=pltpu.VMEM)
    return pl.pallas_call(
        kernel,
        out_shape=[jax.ShapeDtypeStruct(s, d) for s, d in outs],
        in_specs=[vmem] * ins,
        out_specs=[vmem] * len(outs),
        scratch_shapes=scratch,
        compiler_params=pltpu.CompilerParams(**params),
    )


def body(
    forcing, ice_state, sensitivity, owner_device, panel_slot, row_offset,
    intersection_weight, col_map, ocean_mask, lift_weight, conv_weight, conv_bias,
):
    n = lax.axis_size("tile")
    nb = n * BLK
    nk = ROWS_DEV * K
    V, D = pltpu.VMEM, pltpu.SemaphoreType.DMA
    pr = forcing.shape[1]
    own_c = owner_device.reshape(nk, 1)
    own_r = owner_device.reshape(1, nk)
    loc_c = (panel_slot * pr + row_offset).reshape(nk, 1)
    w_c = intersection_weight.reshape(nk, 1)
    forc = forcing.reshape(ROWS_DEV, 2, 5, 128).transpose(1, 0, 2, 3).reshape(2 * ROWS_DEV, HALF)
    pre, oh, w2, iceh, sensh, och = call(
        functools.partial(gather_kernel, n),
        [((128, HALF), bf16), ((nb, 128), bf16), ((64, nb), bf16),
         ((2, 6, 128, 128), bf16), ((2, 3, 128, 128), bf16), ((2, 8, 128), jnp.int32)],
        [V((nb, 128), bf16), V((nb, 128), bf16), V((nb, HALF), bf16), V((nb, HALF), bf16),
         V((64, HALF), bf16), V((128, HALF), bf16),
         D((n,)), D((n,)), D((n,)), D((n,)), D((10,)), D((10,))],
        8, 1,
    )(ice_state, sensitivity, ocean_mask, own_c, own_r, loc_c, w_c, forc)
    lift16 = jnp.pad(lift_weight, ((0, FP - F), (0, 0)))
    field = (E, 128, 128)
    img, sg, terms = call(
        functools.partial(layers_kernel, n),
        [((ROWS_DEV, 128, 128), bf16), ((ROWS_DEV, 128, 128), bf16), ((nb, HALF), bf16)],
        [V((E // 2, 128, 768), bf16), V((E // 2, 128, 768), bf16), V(field, f32), V(field, f32),
         V(field, f32), V(field, f32), V(field, f32), V(field, bf16),
         V((1536, 256), bf16), V((256, 1536), bf16), V((E, 128), f32), V((64, FP, 128), f32),
         V((ROWS_DEV, FP, 128), f32), V((64, HALF), bf16)],
        12,
    )(ice_state, sensitivity, ocean_mask, iceh, sensh, och, pre, col_map, lift16,
      conv_weight.reshape(27, 128, 128), conv_bias, w2)
    (grad,) = call(
        functools.partial(return_kernel, n),
        [((2 * ROWS_DEV, HALF), f32)],
        [V((nb, HALF), bf16), D((n,)), D((n,))],
        2, 2,
    )(terms, oh)
    grad = grad.reshape(2, ROWS_DEV, 5, 128).transpose(1, 0, 2, 3).reshape(forcing.shape)
    return img, sg, grad


def solution(mesh):
    in_specs = (
        P(("member", "tile"), None, None, None),
        P(("member", "tile"), None, None),
        P(("member", "tile"), None, None),
        P("tile", None),
        P("tile", None),
        P("tile", None),
        P("tile", None),
        P(),
        P("tile", None),
        P(),
        P(),
        P(),
    )
    out_specs = (
        P(("member", "tile"), None, None),
        P(("member", "tile"), None, None),
        P(("member", "tile"), None, None, None),
    )
    return jax.shard_map(body, mesh=mesh, in_specs=in_specs, out_specs=out_specs, check_vma=False)
```

```python
import functools

import jax
import jax.numpy as jnp
from jax import lax
from jax.experimental import pallas as pl
from jax.experimental.pallas import tpu as pltpu
from jax.sharding import PartitionSpec as P

F = 10
K = 4
ROWS_DEV = 32
FP = 16
HALF = 640
BLK = 16
E = 48
TRANSPOSED = False
f32, bf16 = jnp.float32, jnp.bfloat16


def dot(a, b, ca=1, cb=0):
    return lax.dot_general(a, b, (((ca,), (cb,)), ((), ())), preferred_element_type=f32)


def iota(shape, dim):
    return lax.broadcasted_iota(jnp.int32, shape, dim)


def remote(src, dst, send, recv, target):
    return pltpu.make_async_remote_copy(
        src_ref=src, dst_ref=dst, send_sem=send, recv_sem=recv,
        device_id={"tile": target}, device_id_type=pl.DeviceIdType.MESH,
    )


def block(ref, p):
    return ref.at[pl.ds(pl.multiple_of(p * BLK, BLK), BLK)]


def exchange(n, me, src, dst, send, recv, start, wait):
    def begin(step, carry):
        to = lax.rem(me + step, n)
        remote(block(src, to), block(dst, me), send.at[step], recv.at[step], to).start()
        return carry

    def finish(step, carry):
        to = lax.rem(me + step, n)
        source = lax.rem(me + n - step, n)
        remote(block(src, to), block(dst, source), send.at[step], recv.at[step], to).wait()
        return carry

    if start:
        lax.fori_loop(1, n, begin, 0)
        mine = pl.ds(pl.multiple_of(me * BLK, BLK), BLK)
        dst[mine, :] = src[mine, :]
    if wait:
        lax.fori_loop(1, n, finish, 0)


def program_kernel(
    n, transposed, ice, sens, ocean, own_t, slot_t, off_t, w_t, forc, col_map, lift, cw, cb,
    img, sg, grad,
    oh_send, oh_recv, f_send, f_recv, t_send, t_recv, f2, pre, prex, iceh, sensh, och,
    xa, xb, s0, s1, s2, mask, g, h3, wf, wb, oc, icr, fg, pr2, icev, sensv, cwv,
    ss1, rs1, ss2, rs2, ss3, rs3, ss4, rs4, ls,
):
    me = lax.axis_index("tile")
    right, left = lax.rem(me + 1, n), lax.rem(me + n - 1, n)
    nb = n * BLK
    nk = ROWS_DEV * K
    load_ice = pltpu.make_async_copy(ice, icev, ls.at[0])
    load_sens = pltpu.make_async_copy(sens, sensv, ls.at[1])
    load_cw = pltpu.make_async_copy(cw, cwv, ls.at[2])
    load_ice.start()
    load_cw.start()
    load_sens.start()
    barrier = pltpu.get_barrier_semaphore()

    def greet(step, carry):
        pl.semaphore_signal(
            barrier, inc=1, device_id={"tile": lax.rem(me + step, n)},
            device_id_type=pl.DeviceIdType.MESH,
        )
        return carry

    lax.fori_loop(1, n, greet, 0)

    eye32 = iota((ROWS_DEV, ROWS_DEV), 0) == iota((ROWS_DEV, ROWS_DEV), 1)

    def column(x):
        return jnp.concatenate(
            [jnp.sum(jnp.where(eye32, x[k : k + 1, :], 0.0), axis=1, keepdims=True) for k in range(K)], axis=0
        )

    own = column(own_t[...].astype(f32))
    loc = column((slot_t[...] * forc.shape[2] + off_t[...]).astype(f32))
    w = column(w_t[...])
    eye = iota((nk, nk), 0) == iota((nk, nk), 1)
    own_row = jnp.sum(jnp.where(eye, own, 0.0), axis=0, keepdims=True)
    earlier = iota((nk, nk), 1) < iota((nk, nk), 0)
    rank = jnp.sum(jnp.where((own == own_row) & earlier, 1.0, 0.0), axis=1, keepdims=True)
    col = (own * BLK + rank).astype(jnp.int32)
    loc = loc.astype(jnp.int32)
    lane = iota((nk, nb), 1)
    pa = jnp.where(col == lane, 1.0, 0.0)
    pb = jnp.where(col + 8 == lane, 1.0, 0.0)
    low = iota((nk, 128), 1)
    la = jnp.where(loc == low, 1.0, 0.0)
    lb = jnp.where(loc + ROWS_DEV == low, 1.0, 0.0)
    oh = dot(pa.astype(bf16), la.astype(bf16), 0, 0) + dot(pb.astype(bf16), lb.astype(bf16), 0, 0)
    oh_send[...] = oh.astype(bf16)
    pl.semaphore_wait(barrier, n - 1)
    exchange(n, me, oh_send, oh_recv, ss1, rs1, True, False)
    halos = []
    for i, (src, dst, rows) in enumerate(((ice, iceh, 6), (ocean, och, 8), (sens, sensh, 3))):
        halos.append(remote(src.at[pl.ds(ROWS_DEV - rows, rows)], dst.at[0], ss3.at[2 * i], rs3.at[2 * i], right))
        halos.append(remote(src.at[pl.ds(0, rows)], dst.at[1], ss3.at[2 * i + 1], rs3.at[2 * i + 1], left))
    for copy in halos:
        copy.start()
    rows = iota((ROWS_DEV, nk), 0)
    pick = jnp.where(lax.rem(iota((ROWS_DEV, nk), 1), ROWS_DEV) == rows, 1.0, 0.0).astype(bf16)
    w2 = jnp.concatenate([dot(pick, (pa * w).astype(bf16)), dot(pick, (pb * w).astype(bf16))], axis=0).astype(bf16)
    for q in range(forc.shape[0]):
        for half in range(2):
            for i in range(5):
                f2[half * 32 + q * 8 : half * 32 + q * 8 + 8, i * 128 : i * 128 + 128] = (
                    forc[q, half * 5 + i].astype(f32)
                )
    exchange(n, me, oh_send, oh_recv, ss1, rs1, False, True)
    f_send[...] = dot(oh_recv[:, : 2 * ROWS_DEV], f2[...].astype(bf16)).astype(bf16)
    exchange(n, me, f_send, f_recv, ss2, rs2, True, False)

    keep_low = jnp.where(me == 0, 0.0, 1.0)
    keep_high = jnp.where(me == n - 1, 0.0, 1.0)
    rows = iota((128, 128), 0)
    diag = jnp.where(rows == iota((128, 128), 1), 1.0, 0.0)
    ones = jnp.ones((128, 128), bf16)
    not_first = rows > 0
    not_last = rows < 127

    def put(dst, pair, half, v):
        at = half * 384
        dst[pair, :, at : at + 128] = jnp.where(not_first, pltpu.roll(v, 1, 0), 0.0).astype(bf16)
        dst[pair, :, at + 128 : at + 256] = v.astype(bf16)
        dst[pair, :, at + 256 : at + 384] = jnp.where(not_last, pltpu.roll(v, 127, 0), 0.0).astype(bf16)

    for copy in halos:
        copy.wait()
    load_ice.wait()
    load_sens.wait()
    load_cw.wait()
    oc[0:8, :] = och[0].astype(f32) * keep_low
    oc[8:40, :] = ocean[...].astype(f32)
    oc[40:48, :] = och[1].astype(f32) * keep_high

    def spread(e, carry):
        mask[e] = dot((diag * oc[pl.ds(e, 1), :]).astype(bf16), ones)
        return carry

    lax.fori_loop(2, 46, spread, 0)

    for i in range(6):
        put(xa, (2 + i) // 2, i % 2, iceh[0, i].astype(f32) * keep_low)
        put(xa, (40 + i) // 2, i % 2, iceh[1, i].astype(f32) * keep_high)

    def fill(q, carry):
        put(xa, q + 4, 0, icev[2 * q].astype(f32))
        put(xa, q + 4, 1, icev[2 * q + 1].astype(f32))
        return carry

    lax.fori_loop(0, ROWS_DEV // 2, fill, 0)
    zero = jnp.zeros((128, 384), bf16)
    xb[1, :, 0:384] = zero
    xb[22, :, 384:768] = zero
    for i in range(3):
        g[5 + i] = sensh[0, i].astype(f32)
        g[40 + i] = sensh[1, i].astype(f32)
    g[43] = jnp.zeros((128, 128), f32)
    g[44] = jnp.zeros((128, 128), f32)

    def fill_g(r, carry):
        g[r + 8] = sensv[r].astype(f32)
        return carry

    lax.fori_loop(0, ROWS_DEV, fill_g, 0)

    for j in range(4):
        for s in range(2):
            if not 0 <= j - s <= 2:
                wf[j * 384 : j * 384 + 384, s * 128 : s * 128 + 128] = jnp.zeros((384, 128), bf16)
                if not transposed:
                    wb[s * 128 : s * 128 + 128, j * 384 : j * 384 + 384] = jnp.zeros((128, 384), bf16)

    def set_forward(layer):
        for j in range(4):
            for s in range(2):
                if 0 <= j - s <= 2:
                    for b in range(3):
                        at = j * 384 + b * 128
                        wf[at : at + 128, s * 128 : s * 128 + 128] = cwv[layer * 9 + (j - s) * 3 + b]

    def set_backward_transposed(layer):
        for a in range(3):
            for b in range(3):
                tile = cwv[layer * 9 + (2 - a) * 3 + 2 - b].T
                for s in range(2):
                    at = (a + s) * 384 + b * 128
                    wf[at : at + 128, s * 128 : s * 128 + 128] = tile

    def set_backward(layer):
        if transposed:
            return set_backward_transposed(layer)
        for j in range(4):
            for s in range(2):
                if 0 <= j - s <= 2:
                    for b in range(3):
                        at = j * 384 + b * 128
                        wb[s * 128 : s * 128 + 128, at : at + 128] = cwv[layer * 9 + (2 - j + s) * 3 + 2 - b]

    def run(x, q_first, pairs, count, forward, finish):
        def chunk(c, carry):
            q0 = q_first + c * pairs
            left = x[pl.ds(q0, pairs)].reshape(pairs * 128, 768)
            right = x[pl.ds(q0 + 1, pairs)].reshape(pairs * 128, 768)
            if forward or transposed:
                acc = dot(left, wf[0:768, :]) + dot(right, wf[768:1536, :])
            else:
                acc = dot(left, wb[:, 0:768], 1, 1) + dot(right, wb[:, 768:1536], 1, 1)
            for i in range(pairs):
                for s in range(2):
                    part = acc[i * 128 : i * 128 + 128, s * 128 : s * 128 + 128]
                    finish(2 * (q0 + i) + 1 + s, q0 + i + s, 1 - s, part)
            return carry

        lax.fori_loop(0, count, chunk, 0)

    def middle(x, pair, half):
        return x[pair, :, half * 384 + 128 : half * 384 + 256].astype(f32)

    def forward_step(layer, x, keep):
        bias = cb[layer : layer + 1, :]

        def step(e, pair, half, acc):
            t = jnp.tanh(acc + bias)
            m = mask[e]
            keep[e] = m * (1.0 - t * t)
            return (middle(x, pair, half) + m * t).astype(bf16)

        return step

    step0, step1, step2 = forward_step(0, xa, s0), forward_step(1, xb, s1), forward_step(2, xa, s2)

    def finish0(e, pair, half, acc):
        h3[e] = step0(e, pair, half, acc)

    set_forward(0)
    run(xa, 1, 7, 3, True, finish0)

    exchange(n, me, f_send, f_recv, ss2, rs2, False, True)
    pre[...] = dot(w2, f_recv[...]).astype(bf16)
    edges = []
    for half in range(2):
        at = half * 64
        low_rows = pre.at[pl.ds(half * ROWS_DEV, 16)]
        high_rows = pre.at[pl.ds(half * ROWS_DEV + 16, 16)]
        edges.append(remote(high_rows, prex.at[pl.ds(half * 32, 16)], ss3.at[6 + 2 * half], rs3.at[6 + 2 * half], right))
        edges.append(remote(low_rows, prex.at[pl.ds(half * 32 + 16, 16)], ss3.at[7 + 2 * half], rs3.at[7 + 2 * half], left))
    for copy in edges:
        copy.start()
    icr[...] = jnp.zeros_like(icr)
    cm = col_map[...].astype(bf16)
    for half in range(2):
        for i in range(5):
            x = pre[half * 32 : half * 32 + 32, i * 128 : i * 128 + 128]
            icr[16:48, half * 5 + i, :] = dot(x, cm)
    lift16 = lift[...]

    def lifted(e):
        return h3[e].astype(f32) + dot(icr[e + 8].astype(bf16), lift16, 0, 0)

    def lift_pair(q, carry):
        put(xb, q, 0, lifted(2 * q))
        put(xb, q, 1, lifted(2 * q + 1))
        return carry

    set_forward(1)
    lax.fori_loop(4, 20, lift_pair, 0)
    for copy in edges:
        copy.wait()
    for half in range(2):
        for i in range(5):
            x = prex[half * 32 : half * 32 + 32, i * 128 : i * 128 + 128]
            y = dot(x, cm)
            icr[0:16, half * 5 + i, :] = y[0:16] * keep_low
            icr[48:64, half * 5 + i, :] = y[16:32] * keep_high
    for e in (3, 4, 5, 6, 7, 40, 41, 42, 43, 44):
        put(xb, e // 2, e % 2, lifted(e))

    def finish1(e, pair, half, acc):
        put(xa, pair, half, step1(e, pair, half, acc).astype(f32))

    def finish2(e, pair, half, acc):
        h3[e] = step2(e, pair, half, acc)
        put(xb, pair, half, g[e] * s2[e])

    def back2(e, pair, half, acc):
        total = g[e] + acc
        g[e] = total
        put(xa, pair, half, total * s1[e])

    def back1(e, pair, half, acc):
        total = g[e] + acc
        g[e] = total
        put(xb, pair, half, total * s0[e])

    def back0(e, pair, half, acc):
        g[e] = g[e] + acc

    run(xb, 1, 7, 3, True, finish1)
    set_forward(2)
    run(xa, 2, 5, 4, True, finish2)
    out_img = pltpu.make_async_copy(h3.at[pl.ds(8, ROWS_DEV)], img, ls.at[3])
    out_img.start()
    set_backward(2)
    run(xb, 2, 5, 4, False, back2)
    set_backward(1)
    run(xa, 3, 6, 3, False, back1)

    def project(r, carry):
        fg[r] = dot(lift16, g[r + 8].astype(bf16), 1, 1)
        return carry

    lax.fori_loop(0, ROWS_DEV, project, 0)
    fg[...] = dot(fg[...].reshape(ROWS_DEV * FP, 128).astype(bf16), cm, 1, 1).reshape(ROWS_DEV, FP, 128)
    for half in range(2):
        for i in range(5):
            pr2[half * 32 : half * 32 + 32, i * 128 : i * 128 + 128] = fg[:, half * 5 + i, :].astype(bf16)
    t_send[...] = dot(w2, pr2[...], 0, 0).astype(bf16)
    exchange(n, me, t_send, t_recv, ss4, rs4, True, False)
    set_backward(0)
    run(xb, 3, 6, 3, False, back0)
    icev[...] = g[8:40].astype(bf16)
    out_sg = pltpu.make_async_copy(icev, sg, ls.at[4])
    out_sg.start()
    exchange(n, me, t_send, t_recv, ss4, rs4, False, True)
    total = dot(oh_recv[:, : 2 * ROWS_DEV], t_recv[...], 0, 0)
    for q in range(grad.shape[0]):
        for half in range(2):
            for i in range(5):
                grad[q, half * 5 + i] = total[half * 32 + q * 8 : half * 32 + q * 8 + 8, i * 128 : i * 128 + 128]
    out_img.wait()
    out_sg.wait()


def body(
    forcing, ice_state, sensitivity, owner_device, panel_slot, row_offset,
    intersection_weight, col_map, ocean_mask, lift_weight, conv_weight, conv_bias,
):
    n = lax.axis_size("tile")
    nb = n * BLK
    V, D = pltpu.VMEM, pltpu.SemaphoreType.DMA
    vmem, hbm = pl.BlockSpec(memory_space=pltpu.VMEM), pl.BlockSpec(memory_space=pl.ANY)
    panels, pr = forcing.shape[:2]
    lift16 = jnp.pad(lift_weight, ((0, FP - F), (0, 0)))
    field = (E, 128, 128)
    tile = (ROWS_DEV, 128, 128)
    img, sg, grad = pl.pallas_call(
        functools.partial(program_kernel, n, TRANSPOSED),
        out_shape=[
            jax.ShapeDtypeStruct(tile, bf16),
            jax.ShapeDtypeStruct(tile, bf16),
            jax.ShapeDtypeStruct((panels, F, pr, 128), f32),
        ],
        in_specs=[hbm, hbm] + [vmem] * 8 + [hbm, vmem],
        out_specs=[hbm, hbm, vmem],
        scratch_shapes=[
            V((nb, 128), bf16), V((nb, 128), bf16), V((nb, HALF), bf16), V((nb, HALF), bf16),
            V((nb, HALF), bf16), V((nb, HALF), bf16), V((64, HALF), f32), V((64, HALF), bf16), V((64, HALF), bf16),
            V((2, 6, 128, 128), bf16), V((2, 3, 128, 128), bf16), V((2, 8, 128), jnp.int32),
            V((E // 2, 128, 768), bf16), V((E // 2, 128, 768), bf16), V(field, f32), V(field, f32),
            V(field, f32), V(field, f32), V(field, f32), V(field, bf16),
            V((1536, 256), bf16), V((256, 1536), bf16), V((E, 128), f32), V((64, FP, 128), f32),
            V((ROWS_DEV, FP, 128), f32), V((64, HALF), bf16), V(tile, bf16), V(tile, bf16), V((27, 128, 128), bf16),
            D((n,)), D((n,)), D((n,)), D((n,)), D((10,)), D((10,)), D((n,)), D((n,)), D((5,)),
        ],
        compiler_params=pltpu.CompilerParams(
            vmem_limit_bytes=56 * 1024 * 1024, collective_id=1, has_side_effects=True
        ),
    )(ice_state, sensitivity, ocean_mask, owner_device.T, panel_slot.T, row_offset.T, intersection_weight.T,
      forcing.transpose(0, 2, 1, 3), col_map, lift16, conv_weight.reshape(27, 128, 128), conv_bias)
    return img, sg, grad.transpose(0, 2, 1, 3)


def solution(mesh):
    in_specs = (
        P(("member", "tile"), None, None, None),
        P(("member", "tile"), None, None),
        P(("member", "tile"), None, None),
        P("tile", None),
        P("tile", None),
        P("tile", None),
        P("tile", None),
        P(),
        P("tile", None),
        P(),
        P(),
        P(),
    )
    out_specs = (
        P(("member", "tile"), None, None),
        P(("member", "tile"), None, None),
        P(("member", "tile"), None, None, None),
    )
    return jax.shard_map(body, mesh=mesh, in_specs=in_specs, out_specs=out_specs, check_vma=False)
```

```python
import functools

import jax
import jax.numpy as jnp
from jax import lax
from jax.experimental import pallas as pl
from jax.experimental.pallas import tpu as pltpu
from jax.sharding import PartitionSpec as P

F = 10
K = 4
ROWS_DEV = 32
FP = 16
HALF = 640
BLK = 16
E = 48
TRANSPOSED = False
f32, bf16 = jnp.float32, jnp.bfloat16


def dot(a, b, ca=1, cb=0):
    return lax.dot_general(a, b, (((ca,), (cb,)), ((), ())), preferred_element_type=f32)


def iota(shape, dim):
    return lax.broadcasted_iota(jnp.int32, shape, dim)


def remote(src, dst, send, recv, target):
    return pltpu.make_async_remote_copy(
        src_ref=src, dst_ref=dst, send_sem=send, recv_sem=recv,
        device_id={"tile": target}, device_id_type=pl.DeviceIdType.MESH,
    )


def block(ref, p):
    return ref.at[pl.ds(pl.multiple_of(p * BLK, BLK), BLK)]


def exchange(n, me, src, dst, send, recv, start, wait):
    def begin(step, carry):
        to = lax.rem(me + step, n)
        remote(block(src, to), block(dst, me), send.at[step], recv.at[step], to).start()
        return carry

    def finish(step, carry):
        to = lax.rem(me + step, n)
        source = lax.rem(me + n - step, n)
        remote(block(src, to), block(dst, source), send.at[step], recv.at[step], to).wait()
        return carry

    if start:
        lax.fori_loop(1, n, begin, 0)
        mine = pl.ds(pl.multiple_of(me * BLK, BLK), BLK)
        dst[mine, :] = src[mine, :]
    if wait:
        lax.fori_loop(1, n, finish, 0)


def program_kernel(
    n, transposed, ice, sens, ocean, own_t, slot_t, off_t, w_t, forc, col_map, lift, cw, cb,
    img, sg, grad,
    oh_send, oh_recv, f_send, f_recv, t_send, t_recv, f2, pre, prex, iceh, sensh, och,
    xa, xb, s0, s1, s2, mask, g, h3, wf, wb, oc, icr, fg, pr2, icev, sensv, cwv, bd,
    ss1, rs1, ss2, rs2, ss3, rs3, ss4, rs4, ls,
):
    me = lax.axis_index("tile")
    right, left = lax.rem(me + 1, n), lax.rem(me + n - 1, n)
    nb = n * BLK
    nk = ROWS_DEV * K
    load_ice = pltpu.make_async_copy(ice, icev, ls.at[0])
    load_sens = pltpu.make_async_copy(sens, sensv, ls.at[1])
    load_cw = pltpu.make_async_copy(cw, cwv, ls.at[2])
    load_ice.start()
    load_cw.start()
    load_sens.start()
    barrier = pltpu.get_barrier_semaphore()

    def greet(step, carry):
        pl.semaphore_signal(
            barrier, inc=1, device_id={"tile": lax.rem(me + step, n)},
            device_id_type=pl.DeviceIdType.MESH,
        )
        return carry

    lax.fori_loop(1, n, greet, 0)

    eye32 = iota((ROWS_DEV, ROWS_DEV), 0) == iota((ROWS_DEV, ROWS_DEV), 1)

    def column(x):
        return jnp.concatenate(
            [jnp.sum(jnp.where(eye32, x[k : k + 1, :], 0.0), axis=1, keepdims=True) for k in range(K)], axis=0
        )

    own = column(own_t[...].astype(f32))
    loc = column((slot_t[...] * forc.shape[2] + off_t[...]).astype(f32))
    w = column(w_t[...])
    eye = iota((nk, nk), 0) == iota((nk, nk), 1)
    own_row = jnp.sum(jnp.where(eye, own, 0.0), axis=0, keepdims=True)
    earlier = iota((nk, nk), 1) < iota((nk, nk), 0)
    rank = jnp.sum(jnp.where((own == own_row) & earlier, 1.0, 0.0), axis=1, keepdims=True)
    col = (own * BLK + rank).astype(jnp.int32)
    loc = loc.astype(jnp.int32)
    lane = iota((nk, nb), 1)
    pa = jnp.where(col == lane, 1.0, 0.0)
    pb = jnp.where(col + 8 == lane, 1.0, 0.0)
    low = iota((nk, 128), 1)
    la = jnp.where(loc == low, 1.0, 0.0)
    lb = jnp.where(loc + ROWS_DEV == low, 1.0, 0.0)
    oh = dot(pa.astype(bf16), la.astype(bf16), 0, 0) + dot(pb.astype(bf16), lb.astype(bf16), 0, 0)
    oh_send[...] = oh.astype(bf16)
    pl.semaphore_wait(barrier, n - 1)
    exchange(n, me, oh_send, oh_recv, ss1, rs1, True, False)
    halos = []
    for i, (src, dst, rows) in enumerate(((ice, iceh, 6), (ocean, och, 8), (sens, sensh, 3))):
        halos.append(remote(src.at[pl.ds(ROWS_DEV - rows, rows)], dst.at[0], ss3.at[2 * i], rs3.at[2 * i], right))
        halos.append(remote(src.at[pl.ds(0, rows)], dst.at[1], ss3.at[2 * i + 1], rs3.at[2 * i + 1], left))
    for copy in halos:
        copy.start()
    rows = iota((ROWS_DEV, nk), 0)
    pick = jnp.where(lax.rem(iota((ROWS_DEV, nk), 1), ROWS_DEV) == rows, 1.0, 0.0).astype(bf16)
    w2 = jnp.concatenate([dot(pick, (pa * w).astype(bf16)), dot(pick, (pb * w).astype(bf16))], axis=0).astype(bf16)
    for q in range(forc.shape[0]):
        for half in range(2):
            for i in range(5):
                f2[half * 32 + q * 8 : half * 32 + q * 8 + 8, i * 128 : i * 128 + 128] = (
                    forc[q, half * 5 + i].astype(f32)
                )
    exchange(n, me, oh_send, oh_recv, ss1, rs1, False, True)
    f_send[...] = dot(oh_recv[:, : 2 * ROWS_DEV], f2[...].astype(bf16)).astype(bf16)
    exchange(n, me, f_send, f_recv, ss2, rs2, True, False)

    keep_low = jnp.where(me == 0, 0.0, 1.0)
    keep_high = jnp.where(me == n - 1, 0.0, 1.0)
    rows = iota((128, 128), 0)
    diag = jnp.where(rows == iota((128, 128), 1), 1.0, 0.0)
    ones = jnp.ones((128, 128), bf16)
    not_first = rows > 0
    not_last = rows < 127

    def put(dst, pair, half, v):
        at = half * 384
        dst[pair, :, at : at + 128] = jnp.where(not_first, pltpu.roll(v, 1, 0), 0.0).astype(bf16)
        dst[pair, :, at + 128 : at + 256] = v.astype(bf16)
        dst[pair, :, at + 256 : at + 384] = jnp.where(not_last, pltpu.roll(v, 127, 0), 0.0).astype(bf16)

    for copy in halos:
        copy.wait()
    load_ice.wait()
    load_sens.wait()
    load_cw.wait()
    oc[0:8, :] = och[0].astype(f32) * keep_low
    oc[8:40, :] = ocean[...].astype(f32)
    oc[40:48, :] = och[1].astype(f32) * keep_high

    def spread(c, carry):
        e = 8 * c
        cells = oc[pl.ds(pl.multiple_of(e, 8), 8), :]
        wide = jnp.concatenate([(diag * cells[i : i + 1, :]).astype(bf16) for i in range(8)], axis=0)
        mask[pl.ds(e, 8)] = dot(wide, ones).reshape(8, 128, 128)
        return carry

    lax.fori_loop(0, E // 8, spread, 0)

    for i in range(6):
        put(xa, (2 + i) // 2, i % 2, iceh[0, i].astype(f32) * keep_low)
        put(xa, (40 + i) // 2, i % 2, iceh[1, i].astype(f32) * keep_high)

    def fill(q, carry):
        put(xa, q + 4, 0, icev[2 * q].astype(f32))
        put(xa, q + 4, 1, icev[2 * q + 1].astype(f32))
        return carry

    lax.fori_loop(0, ROWS_DEV // 2, fill, 0)
    zero = jnp.zeros((128, 384), bf16)
    xb[1, :, 0:384] = zero
    xb[22, :, 384:768] = zero
    for i in range(3):
        g[5 + i] = sensh[0, i].astype(f32)
        g[40 + i] = sensh[1, i].astype(f32)
    g[43] = jnp.zeros((128, 128), f32)
    g[44] = jnp.zeros((128, 128), f32)

    def fill_g(r, carry):
        g[r + 8] = sensv[r].astype(f32)
        return carry

    lax.fori_loop(0, ROWS_DEV, fill_g, 0)

    for j in range(4):
        for s in range(2):
            if not 0 <= j - s <= 2:
                wf[j * 384 : j * 384 + 384, s * 128 : s * 128 + 128] = jnp.zeros((384, 128), bf16)
                if not transposed:
                    wb[s * 128 : s * 128 + 128, j * 384 : j * 384 + 384] = jnp.zeros((128, 384), bf16)

    def set_forward(layer):
        for j in range(4):
            for s in range(2):
                if 0 <= j - s <= 2:
                    for b in range(3):
                        at = j * 384 + b * 128
                        wf[at : at + 128, s * 128 : s * 128 + 128] = cwv[layer * 9 + (j - s) * 3 + b]

    def set_backward_transposed(layer):
        for a in range(3):
            for b in range(3):
                tile = cwv[layer * 9 + (2 - a) * 3 + 2 - b].T
                for s in range(2):
                    at = (a + s) * 384 + b * 128
                    wf[at : at + 128, s * 128 : s * 128 + 128] = tile

    def set_backward(layer):
        if transposed:
            return set_backward_transposed(layer)
        for j in range(4):
            for s in range(2):
                if 0 <= j - s <= 2:
                    for b in range(3):
                        at = j * 384 + b * 128
                        wb[s * 128 : s * 128 + 128, at : at + 128] = cwv[layer * 9 + (2 - j + s) * 3 + 2 - b]

    def run(x, q_first, pairs, count, forward, finish):
        def chunk(c, carry):
            q0 = q_first + c * pairs
            left = x[pl.ds(q0, pairs)].reshape(pairs * 128, 768)
            right = x[pl.ds(q0 + 1, pairs)].reshape(pairs * 128, 768)
            if forward or transposed:
                acc = dot(left, wf[0:768, :]) + dot(right, wf[768:1536, :])
            else:
                acc = dot(left, wb[:, 0:768], 1, 1) + dot(right, wb[:, 768:1536], 1, 1)
            for i in range(pairs):
                for s in range(2):
                    part = acc[i * 128 : i * 128 + 128, s * 128 : s * 128 + 128]
                    finish(2 * (q0 + i) + 1 + s, q0 + i + s, 1 - s, part)
            return carry

        lax.fori_loop(0, count, chunk, 0, unroll=True)

    def middle(x, pair, half):
        return x[pair, :, half * 384 + 128 : half * 384 + 256].astype(f32)

    def forward_step(layer, x, keep):
        bias = cb[layer : layer + 1, :]

        def step(e, pair, half, acc):
            t = jnp.tanh(acc + bias)
            m = mask[e]
            keep[e] = m * (1.0 - t * t)
            return (middle(x, pair, half) + m * t).astype(bf16)

        return step

    step0, step1, step2 = forward_step(0, xa, s0), forward_step(1, xb, s1), forward_step(2, xa, s2)

    def finish0(e, pair, half, acc):
        h3[e] = step0(e, pair, half, acc)

    set_forward(0)
    run(xa, 1, 7, 3, True, finish0)

    exchange(n, me, f_send, f_recv, ss2, rs2, False, True)
    pre[...] = dot(w2, f_recv[...]).astype(bf16)
    edges = []
    for half in range(2):
        at = half * 64
        low_rows = pre.at[pl.ds(half * ROWS_DEV, 16)]
        high_rows = pre.at[pl.ds(half * ROWS_DEV + 16, 16)]
        edges.append(remote(high_rows, prex.at[pl.ds(half * 32, 16)], ss3.at[6 + 2 * half], rs3.at[6 + 2 * half], right))
        edges.append(remote(low_rows, prex.at[pl.ds(half * 32 + 16, 16)], ss3.at[7 + 2 * half], rs3.at[7 + 2 * half], left))
    for copy in edges:
        copy.start()
    icr[...] = jnp.zeros_like(icr)
    cm = col_map[...].astype(bf16)
    for half in range(2):
        for i in range(5):
            x = pre[half * 32 : half * 32 + 32, i * 128 : i * 128 + 128]
            icr[16:48, half * 5 + i, :] = dot(x, cm)
    lift16 = lift[...]

    eight = jnp.concatenate([lift16] * 8, axis=0)
    of_row = iota((128, 128), 0) // FP
    for i in range(8):
        bd[:, i * 128 : i * 128 + 128] = jnp.where(of_row == i, eight, jnp.zeros_like(eight))

    def lift_eight(c, chosen):
        wide = dot(icr[pl.ds(8 * c + 8, 8)].reshape(8 * FP, 128).astype(bf16), bd[...], 0, 0)
        for i in chosen:
            v = h3[8 * c + i].astype(f32) + wide[:, i * 128 : i * 128 + 128]
            put(xb, 4 * c + i // 2, i % 2, v)

    def lift_inner(c, carry):
        lift_eight(c, range(8))
        return carry

    set_forward(1)
    lax.fori_loop(1, 5, lift_inner, 0)
    for copy in edges:
        copy.wait()
    for half in range(2):
        for i in range(5):
            x = prex[half * 32 : half * 32 + 32, i * 128 : i * 128 + 128]
            y = dot(x, cm)
            icr[0:16, half * 5 + i, :] = y[0:16] * keep_low
            icr[48:64, half * 5 + i, :] = y[16:32] * keep_high
    lift_eight(0, range(3, 8))
    lift_eight(5, range(5))

    def finish1(e, pair, half, acc):
        put(xa, pair, half, step1(e, pair, half, acc).astype(f32))

    def finish2(e, pair, half, acc):
        h3[e] = step2(e, pair, half, acc)
        put(xb, pair, half, g[e] * s2[e])

    def back2(e, pair, half, acc):
        total = g[e] + acc
        g[e] = total
        put(xa, pair, half, total * s1[e])

    def back1(e, pair, half, acc):
        total = g[e] + acc
        g[e] = total
        put(xb, pair, half, total * s0[e])

    def back0(e, pair, half, acc):
        g[e] = g[e] + acc

    run(xb, 1, 7, 3, True, finish1)
    set_forward(2)
    run(xa, 2, 5, 4, True, finish2)
    img[...] = h3[8:40]
    set_backward(2)
    run(xb, 2, 5, 4, False, back2)
    set_backward(1)
    run(xa, 3, 6, 3, False, back1)

    def project(c, carry):
        wide = jnp.concatenate([g[8 * c + 8 + i].astype(bf16) for i in range(8)], axis=1)
        fg[pl.ds(8 * c, 8)] = dot(bd[...], wide, 1, 1).reshape(8, FP, 128)
        return carry

    lax.fori_loop(0, ROWS_DEV // 8, project, 0)
    fg[...] = dot(fg[...].reshape(ROWS_DEV * FP, 128).astype(bf16), cm, 1, 1).reshape(ROWS_DEV, FP, 128)
    for half in range(2):
        for i in range(5):
            pr2[half * 32 : half * 32 + 32, i * 128 : i * 128 + 128] = fg[:, half * 5 + i, :].astype(bf16)
    t_send[...] = dot(w2, pr2[...], 0, 0).astype(bf16)
    exchange(n, me, t_send, t_recv, ss4, rs4, True, False)
    set_backward(0)
    run(xb, 3, 6, 3, False, back0)
    sg[...] = g[8:40].astype(bf16)
    exchange(n, me, t_send, t_recv, ss4, rs4, False, True)
    total = dot(oh_recv[:, : 2 * ROWS_DEV], t_recv[...], 0, 0)
    for q in range(grad.shape[0]):
        for half in range(2):
            for i in range(5):
                grad[q, half * 5 + i] = total[half * 32 + q * 8 : half * 32 + q * 8 + 8, i * 128 : i * 128 + 128]


def body(
    forcing, ice_state, sensitivity, owner_device, panel_slot, row_offset,
    intersection_weight, col_map, ocean_mask, lift_weight, conv_weight, conv_bias,
):
    n = lax.axis_size("tile")
    nb = n * BLK
    V, D = pltpu.VMEM, pltpu.SemaphoreType.DMA
    vmem, hbm = pl.BlockSpec(memory_space=pltpu.VMEM), pl.BlockSpec(memory_space=pl.ANY)
    panels, pr = forcing.shape[:2]
    lift16 = jnp.pad(lift_weight, ((0, FP - F), (0, 0)))
    field = (E, 128, 128)
    tile = (ROWS_DEV, 128, 128)
    img, sg, grad = pl.pallas_call(
        functools.partial(program_kernel, n, TRANSPOSED),
        out_shape=[
            jax.ShapeDtypeStruct(tile, bf16),
            jax.ShapeDtypeStruct(tile, bf16),
            jax.ShapeDtypeStruct((panels, F, pr, 128), f32),
        ],
        in_specs=[hbm, hbm] + [vmem] * 8 + [hbm, vmem],
        out_specs=[vmem, vmem, vmem],
        scratch_shapes=[
            V((nb, 128), bf16), V((nb, 128), bf16), V((nb, HALF), bf16), V((nb, HALF), bf16),
            V((nb, HALF), bf16), V((nb, HALF), bf16), V((64, HALF), f32), V((64, HALF), bf16), V((64, HALF), bf16),
            V((2, 6, 128, 128), bf16), V((2, 3, 128, 128), bf16), V((2, 8, 128), jnp.int32),
            V((E // 2, 128, 768), bf16), V((E // 2, 128, 768), bf16), V(field, f32), V(field, f32),
            V(field, f32), V(field, f32), V(field, f32), V(field, bf16),
            V((1536, 256), bf16), V((256, 1536), bf16), V((E, 128), f32), V((64, FP, 128), f32),
            V((ROWS_DEV, FP, 128), f32), V((64, HALF), bf16), V(tile, bf16), V(tile, bf16), V((27, 128, 128), bf16), V((128, 1024), bf16),
            D((n,)), D((n,)), D((n,)), D((n,)), D((10,)), D((10,)), D((n,)), D((n,)), D((3,)),
        ],
        compiler_params=pltpu.CompilerParams(
            vmem_limit_bytes=56 * 1024 * 1024, collective_id=1, has_side_effects=True
        ),
    )(ice_state, sensitivity, ocean_mask, owner_device.T, panel_slot.T, row_offset.T, intersection_weight.T,
      forcing.transpose(0, 2, 1, 3), col_map, lift16, conv_weight.reshape(27, 128, 128), conv_bias)
    return img, sg, grad.transpose(0, 2, 1, 3)


def solution(mesh):
    in_specs = (
        P(("member", "tile"), None, None, None),
        P(("member", "tile"), None, None),
        P(("member", "tile"), None, None),
        P("tile", None),
        P("tile", None),
        P("tile", None),
        P("tile", None),
        P(),
        P("tile", None),
        P(),
        P(),
        P(),
    )
    out_specs = (
        P(("member", "tile"), None, None),
        P(("member", "tile"), None, None),
        P(("member", "tile"), None, None, None),
    )
    return jax.shard_map(body, mesh=mesh, in_specs=in_specs, out_specs=out_specs, check_vma=False)
```
